512 devices in a mesh: blk: 64 (over z, y_hi, core), lane: 8 (over x, y_lo).
Axes of the slice: x: 4, y: 8 (y_hi: 4, y_lo: 2; y = y_hi * 2 + y_lo), z: 8, core: 2. Of those that a mesh axis runs over, the one named last changes fastest.
Arguments:
- waves: float32 [8192, 2048], P('blk'), may hold values from -6 to 6
- pair_bins: int32 [8192, 3, 128], P('blk'), may hold values from 0 to 15
- tile_perm: int32 [64, 64], P('blk'), may hold values from 0 to 63, each once within a row
Outputs:
- gathers: float32 [64, 128, 16, 128], P('blk', 'lane')
The draws below stay inside these ranges and needn't reach their ends.
Inputs may be any that keep to these rules, and one draw needn't show every extreme that they name: Each row of tile_perm is a permutation of 0 to 64 - 1.
All inputs are finite; a program needn't handle non-finite values.
Results may differ from the reference program's by a relative error of at most 0.0039.
Values may be sent and summed in bfloat16 or wider, within the bound.
No kernel may reach another device: no remote copies, remote signals or barrier semaphores. Data moves between devices by JAX's collectives and lax.ppermute only.
A program may use at most 64 MiB of HBM per device.

```python
import jax
import jax.numpy as jnp
from jax import lax

S = 2048
LAGS = 64
NBIN = 16
BLOCK = 128
STEPS = 3
NODES = 8192
TS = 2
N_BLK = 64


def plant(drawn, own_key, least, largest):
    shape = drawn.shape
    place = [jax.random.randint(jax.random.fold_in(own_key, axis), (), 0, shape[axis]) for axis in range(len(shape))]
    drawn = drawn.at[tuple(place)].set(least)
    longest = shape.index(max(shape))
    place[longest] = (place[longest] + 1) % shape[longest]
    return drawn.at[tuple(place)].set(largest)


def block_scale(key, extent, cuts, least, high):
    factor_of = 1.0
    for axis_at, blocks in cuts:
        steps = jax.random.uniform(jax.random.fold_in(jax.random.fold_in(key, 6), axis_at), (blocks,), jnp.float32, least / len(cuts), high / len(cuts))
        factor_of = factor_of * jnp.repeat(jnp.exp(steps), extent[axis_at] // blocks).reshape((-1,) + (1,) * (len(extent) - 1 - axis_at))
    return factor_of


def scatter_about(stream_key, extent, width, limit, cuts=(), kind=jnp.bfloat16):
    loudness = block_scale(stream_key, extent, cuts, -0.22, 0.18) if cuts else 1.0
    values = jax.random.normal(stream_key, extent, jnp.float32) * width * loudness
    return jnp.minimum(jnp.maximum(values, -limit), limit).astype(kind)


def setup_inputs(seed: int = 0) -> dict:
    splits = jax.random.split(jax.random.key(seed), 4)
    return {
        "waves": scatter_about(splits[0], (NODES, S), 1.0, 6.0, ((0, 64),), jnp.float32),
        "pair_bins": plant(jax.random.randint(splits[1], (NODES, STEPS, BLOCK), 0, NBIN), jax.random.fold_in(splits[1], 1), 0, NBIN - 1).astype(jnp.int32),
        "tile_perm": jax.vmap(lambda own: jax.random.permutation(own, N_BLK))(jax.random.split(splits[2], N_BLK)).reshape((N_BLK, N_BLK)).astype(jnp.int32),
    }


def lagged_products(source_rows, guest_padded):
    layers = []
    for lag_index in range(LAGS):
        shifted = guest_padded[:, lag_index:lag_index + S]
        layers.append(lax.dot_general(source_rows, shifted, (((1,), (1,)), ((), ())), preferred_element_type=jnp.float32))
    return jnp.stack(layers, axis=2) / S

def reference(waves, pair_bins, tile_perm):
    row_norms = jnp.sqrt(lax.optimization_barrier(jnp.mean(waves * waves, axis=1, keepdims=True)) + 1e-06)
    normed = (waves / row_norms).astype(jnp.bfloat16)
    blocks = normed.reshape(N_BLK, BLOCK, S)
    padded = jnp.concatenate([blocks, jnp.zeros((N_BLK, BLOCK, LAGS), jnp.bfloat16)], axis=2)
    bin_blocks = pair_bins.reshape(N_BLK, BLOCK, STEPS, BLOCK)
    levels = jnp.arange(NBIN, dtype=jnp.int32)

    def visit(negative, block_index):
        source_rows = blocks[block_index]
        positive = jnp.zeros((BLOCK, NBIN, LAGS), jnp.float32)
        for step_index in range(STEPS):
            guest_index = ((block_index - step_index) % N_BLK).astype(jnp.int32)
            guest_padded = lax.dynamic_index_in_dim(padded, guest_index, 0, keepdims=False)
            products = lagged_products(source_rows, guest_padded)
            bin_onehot = (bin_blocks[block_index][:, step_index, :, None] == levels).astype(jnp.float32)
            positive = positive + jnp.einsum('imb,imk->ibk', bin_onehot, products, precision=lax.Precision.HIGHEST)
            backward = jnp.einsum('imb,imk->mbk', bin_onehot, products, precision=lax.Precision.HIGHEST)
            current = lax.dynamic_index_in_dim(negative, guest_index, 0, keepdims=False)
            negative = lax.dynamic_update_index_in_dim(negative, current + backward, guest_index, 0)
        return (negative, positive)
    start = jnp.zeros((N_BLK, BLOCK, NBIN, LAGS), jnp.float32)
    negative, positive = lax.scan(visit, start, jnp.arange(N_BLK, dtype=jnp.int32))
    both_signs = jnp.stack([positive, negative], axis=3)
    tile_stack = both_signs.reshape(N_BLK, N_BLK, TS, NBIN, 2, LAGS)
    sources = jnp.arange(N_BLK, dtype=jnp.int32)[None, :]
    picked = tile_stack[sources, tile_perm.T]
    return picked.reshape(N_BLK, N_BLK * TS, NBIN, 2 * LAGS)
```

```python
import jax
import jax.numpy as jnp
from jax import lax
from jax.experimental import pallas as pl
from jax.experimental.pallas import tpu as pltpu
from jax.sharding import PartitionSpec as P

S = 2048
LAGS = 64
NBIN = 16
STEPS = 3
BLOCK = 128
GROUPS = 8
PAD = S + 128
WIDE = S + 2 * BLOCK
BF = jnp.bfloat16
F32 = jnp.float32
AXES = ("blk", "lane")


def device(z, h, core, x, y):
    return ((z % 8) * 8 + h * 2 + core) * 8 + x * 2 + y


PLACES = [
    (z, h, c, x, y)
    for z in range(8)
    for h in range(4)
    for c in range(2)
    for x in range(4)
    for y in range(2)
]


def beside(z, h, step):
    chip = (z * 4 + h + step) % 32
    return chip // 4, chip % 4


ACROSS = [
    (device(*pos), device(*beside(pos[0], pos[1], 1 if pos[4] else -1), pos[2], pos[3], 1 - pos[4]))
    for pos in PLACES
]
PARTNER = [(device(*pos), device(pos[0], pos[1], 1 - pos[2], pos[3], pos[4])) for pos in PLACES]
TURN = [
    (device(z, h, c, x, y), device(2 * x + y, h, c, z // 2, z % 2)) for z, h, c, x, y in PLACES
]
ROUND = [
    [device(z, h, c, x, y) for y in range(2) for h in range(4) for c in range(2)]
    for z in range(8)
    for x in range(4)
]


def dot(a, b):
    return lax.dot_general(a, b, (((1,), (0,)), ((), ())), preferred_element_type=F32)


def prepare(waves_ref, bins_ref, load_ref, own_ref):
    for r in range(0, BLOCK, 32):
        w = waves_ref[r : r + 32, :]
        norm = jnp.sqrt(jnp.mean(w * w, axis=1, keepdims=True) + 1e-06)
        load_ref[r : r + 32, :S] = (w / norm).astype(BF)
    for s in range(STEPS):
        b = bins_ref[s].astype(F32)
        turned = jnp.transpose(b).astype(BF)
        own_ref[s] = b.astype(BF)
        if s == 0:
            own_ref[STEPS] = turned
        else:
            load_ref[:, S + (s - 1) * BLOCK : S + s * BLOCK] = turned


def toeplitz(place_ref, perm_ref, load_ref, out_ref, pick_ref):
    g = pl.program_id(0)
    tiles = [perm_ref[0, place_ref[1] + 2 * g + own] * 2 for own in range(2)]
    node = [tiles[i % 2] + i // 2 for i in range(4)]

    def chosen(rows, which):
        at = which(lax.broadcasted_iota(jnp.int32, (rows, BLOCK), 0))
        want = jnp.where(at < 2, jnp.where(at == 0, node[0], node[1]), jnp.where(at == 2, node[2], node[3]))
        return (lax.broadcasted_iota(jnp.int32, (rows, BLOCK), 1) == want).astype(BF)

    pick_ref[...] = chosen(64, lambda r: r // NBIN)
    x = dot(chosen(16, lambda r: r % 4), load_ref[:, :S])
    x = jnp.concatenate([x, jnp.zeros((16, PAD - S), F32)], axis=1)
    x = jnp.where(place_ref[0] == 0, pltpu.roll(x, LAGS - 1, 1), x)
    row = lax.broadcasted_iota(jnp.int32, (16, PAD), 0) // 4
    base = x
    for kk in range(1, 4):
        base = jnp.where(row == kk, pltpu.roll(x, PAD - kk, 1), base)
    for q in range(16):
        moved = base if q == 0 else pltpu.roll(base, PAD - 4 * q, 1)
        out_ref[0, q * 16 : (q + 1) * 16, :] = moved[:, :S].astype(BF)


def correlate(place_ref, pick_ref, own_ref, load_ref, far_ref, near_ref, shift_ref, out_ref, sums_ref):
    g = pl.program_id(0)
    rows = GROUPS * 64

    @pl.when(g == 0)
    def _():
        level = (lax.broadcasted_iota(jnp.int32, (rows, BLOCK), 0) % NBIN).astype(F32)
        forward = place_ref[0] == 0
        pick = pick_ref[...]
        tables = (
            jnp.where(forward, own_ref[0], own_ref[3]),
            jnp.where(forward, own_ref[1], near_ref[:, S : S + BLOCK]),
            jnp.where(forward, own_ref[2], far_ref[:, S + BLOCK :]),
        )
        hot = [(dot(pick, t) == level).astype(BF) for t in tables]
        for n in range(0, S, 256):
            at = slice(n, n + 256)
            v = dot(hot[0], load_ref[:, at]) + dot(hot[2], far_ref[:, at]) + dot(hot[1], near_ref[:, at])
            top = v.astype(BF)
            rest = (v - top.astype(F32)).astype(BF)
            sums_ref[:, 0:64, at] = top.reshape(GROUPS, 64, 256)
            sums_ref[:, 64:128, at] = rest.reshape(GROUPS, 64, 256)

    full = lax.dot_general(
        sums_ref[g], shift_ref[0], (((1,), (1,)), ((), ())), preferred_element_type=F32
    )
    c = (full[0:64] + full[64:128]) * (1.0 / S)
    r = lax.broadcasted_iota(jnp.int32, (64, 256), 0) // 16
    k = lax.broadcasted_iota(jnp.int32, (64, 256), 1) % 4
    c = jnp.where(r == k, c, 0.0).astype(BF)
    lag = lax.broadcasted_iota(jnp.int32, (256, 128), 0) // 4
    col = lax.broadcasted_iota(jnp.int32, (256, 128), 1)
    first = (lag == col).astype(BF)
    second = (lag + LAGS == col).astype(BF)
    out = dot(c[0:32], first) + dot(c[32:64], second)
    out_ref[...] = out.astype(BF).reshape(2, NBIN, 128)


def assemble(y_ref, out_ref):
    i = lax.broadcasted_iota(jnp.int32, (128, 256), 0)
    o = lax.broadcasted_iota(jnp.int32, (128, 256), 1)
    same = (i // LAGS) == (o // 128)
    early = jnp.logical_and(same, o % 128 == LAGS - 1 - i % LAGS).astype(BF)
    late = jnp.logical_and(same, o % 128 == LAGS + i % LAGS).astype(BF)
    out = dot(y_ref[0:8].reshape(128, 128), early) + dot(y_ref[8:16].reshape(128, 128), late)
    for q in range(2):
        out_ref[:, q] = out[:, q * 128 : (q + 1) * 128].reshape(8, NBIN, 128)


def whole(shape):
    return pl.BlockSpec(shape, lambda *_: (0,) * len(shape))


SCALAR = pl.BlockSpec(memory_space=pltpu.SMEM)


def limit(mib):
    return pltpu.CompilerParams(vmem_limit_bytes=mib << 20)


def on_device(waves, pair_bins, tile_perm):
    core = lax.axis_index("blk") % 2
    lane = lax.axis_index("lane")
    x, y = lane // 2, lane % 2
    place = jnp.stack([y, x * 16])

    load, own = pl.pallas_call(
        prepare,
        out_shape=(
            jax.ShapeDtypeStruct((BLOCK, WIDE), BF),
            jax.ShapeDtypeStruct((4, BLOCK, BLOCK), BF),
        ),
        compiler_params=limit(16),
        name="prepare",
    )(waves, jnp.transpose(pair_bins, (1, 0, 2)))

    far = lax.ppermute(load, AXES, ACROSS)

    shifts, pick = pl.pallas_call(
        toeplitz,
        grid=(GROUPS,),
        in_specs=[SCALAR, SCALAR, whole((BLOCK, WIDE))],
        out_specs=(
            pl.BlockSpec((1, 256, S), lambda g: (g, 0, 0)),
            pl.BlockSpec((64, BLOCK), lambda g: (g, 0)),
        ),
        out_shape=(
            jax.ShapeDtypeStruct((GROUPS, 256, S), BF),
            jax.ShapeDtypeStruct((GROUPS * 64, BLOCK), BF),
        ),
        compiler_params=limit(16),
        cost_estimate=pl.CostEstimate(flops=2 * 128 * 128 * S, bytes_accessed=GROUPS * 512 * S, transcendentals=0),
        name="toeplitz",
    )(place, tile_perm, load)
    far, shifts, pick = lax.optimization_barrier((far, shifts, pick))

    near = lax.ppermute(jnp.where(core == y, load, far), AXES, PARTNER)

    mine = pl.pallas_call(
        correlate,
        grid=(GROUPS,),
        in_specs=[
            SCALAR,
            whole((GROUPS * 64, BLOCK)),
            whole((4, BLOCK, BLOCK)),
            whole((BLOCK, WIDE)),
            whole((BLOCK, WIDE)),
            whole((BLOCK, WIDE)),
            pl.BlockSpec((1, 256, S), lambda g: (g, 0, 0)),
        ],
        out_specs=pl.BlockSpec((2, NBIN, 128), lambda g: (g, 0, 0)),
        out_shape=jax.ShapeDtypeStruct((16, NBIN, 128), BF),
        scratch_shapes=[pltpu.VMEM((GROUPS, 128, S), BF)],
        compiler_params=limit(32),
        name="correlate",
    )(place, pick, own, load, far, near, shifts)

    mine = lax.all_to_all(mine, AXES, 0, 0, axis_index_groups=ROUND, tiled=True)
    mine = lax.ppermute(mine, AXES, TURN)
    out = pl.pallas_call(
        assemble,
        out_shape=jax.ShapeDtypeStruct((8, 2, NBIN, 128), F32),
        compiler_params=limit(16),
        name="assemble",
    )(mine)
    return out.reshape(1, 16, NBIN, 128)


def solution(mesh):
    placed = (P("blk", None), P("blk", None, None), P("blk", None))
    return jax.shard_map(
        on_device,
        mesh=mesh,
        in_specs=placed,
        out_specs=P("blk", "lane", None, None),
        check_vma=False,
    )
```

```python
import jax
import jax.numpy as jnp
from jax import lax
from jax.experimental import pallas as pl
from jax.experimental.pallas import tpu as pltpu
from jax.sharding import PartitionSpec as P

S = 2048
LAGS = 64
NBIN = 16
STEPS = 3
BLOCK = 128
GROUPS = 16
ROWS = GROUPS * 64
HALF = S // 2
PAD = HALF + 128
WIDE = HALF + 2 * BLOCK
BF = jnp.bfloat16
F32 = jnp.float32
AXES = ("blk", "lane")


def device(z, h, core, x, y):
    return ((z % 8) * 8 + h * 2 + core) * 8 + x * 2 + y


PLACES = [
    (z, h, c, x, y)
    for z in range(8)
    for h in range(4)
    for c in range(2)
    for x in range(4)
    for y in range(2)
]


def beside(z, h, step):
    chip = (z * 4 + h + step) % 32
    return chip // 4, chip % 4


ACROSS = [
    (device(*pos), device(*beside(pos[0], pos[1], 1 if pos[4] else -1), pos[2], pos[3], 1 - pos[4]))
    for pos in PLACES
]
PARTNER = [(device(*pos), device(pos[0], pos[1], 1 - pos[2], pos[3], pos[4])) for pos in PLACES]


def ring(a, b, n):
    return min((a - b) % n, (b - a) % n)


OFFSETS = 0x72016534


def owner_z(z, x, y):
    near = ((x + 4 - (z >> 1)) & 3) * 2 + ((y + z) & 1)
    return (z + ((OFFSETS >> (4 * near)) & 7)) & 7


TURN = [
    (device(z, h, c, x, y), device(owner_z(z, x, y), h, c, z // 2, z % 2))
    for z, h, c, x, y in PLACES
]
ROUND = [
    [
        device(z, h, c, 2 * pair + x, y)
        for x in range(2)
        for y in range(2)
        for h in range(4)
        for c in range(2)
    ]
    for z in range(8)
    for pair in range(2)
]


def dot(a, b):
    return lax.dot_general(a, b, (((1,), (0,)), ((), ())), preferred_element_type=F32)


def prepare(lane_ref, waves_ref, bins_ref, load_ref, full_ref, own_ref):
    low = (lane_ref[0] & 2) == 0
    for r in range(0, BLOCK, 32):
        w = waves_ref[r : r + 32, :]
        norm = jnp.sqrt(jnp.mean(w * w, axis=1, keepdims=True) + 1e-06)
        w = w / norm
        full_ref[r : r + 32, :] = w.astype(BF)
        load_ref[r : r + 32, :HALF] = jnp.where(low, w[:, :HALF], w[:, HALF:]).astype(BF)
    for s in range(STEPS):
        b = bins_ref[s].astype(F32)
        turned = jnp.transpose(b).astype(BF)
        own_ref[s] = b.astype(BF)
        if s == 0:
            own_ref[STEPS] = turned
        else:
            load_ref[:, HALF + (s - 1) * BLOCK : HALF + s * BLOCK] = turned


def one_hot(pick, table):
    level = (lax.broadcasted_iota(jnp.int32, (ROWS, BLOCK), 0) % NBIN).astype(F32)
    return (dot(pick, table) == level).astype(BF)


def early(lane_ref, blk_ref, perm_ref, full_ref, load_ref, own_ref, out_ref, pick_ref, base_ref, rows_ref):
    def chosen(g, rows, which):
        at = which(lax.broadcasted_iota(jnp.int32, (rows, BLOCK), 0))
        first = 8 * owner_z(blk_ref[0] >> 3, ((lane_ref[0] >> 2) << 1) + g // 8, g // 4 % 2) + 2 * (g % 4)
        tiles = [perm_ref[0, first + own] * 2 for own in range(2)]
        node = [tiles[i % 2] + i // 2 for i in range(4)]
        want = jnp.where(at < 2, jnp.where(at == 0, node[0], node[1]), jnp.where(at == 2, node[2], node[3]))
        return (lax.broadcasted_iota(jnp.int32, (rows, BLOCK), 1) == want).astype(BF)

    for g in range(GROUPS):
        pick_ref[g * 64 : (g + 1) * 64, :] = chosen(g, 64, lambda r: r // NBIN)
    few = jnp.concatenate([chosen(g, 16, lambda r: r % 4) for g in range(GROUPS)], axis=0)
    x = dot(few, full_ref[...])
    x = jnp.concatenate([x, jnp.zeros((GROUPS * 16, 128), F32)], axis=1)
    x = jnp.where((lane_ref[0] & 1) == 0, pltpu.roll(x, LAGS - 1, 1), x)
    x = jnp.where((lane_ref[0] & 2) == 0, x[:, :PAD], x[:, HALF:])
    row = lax.broadcasted_iota(jnp.int32, (GROUPS * 16, PAD), 0) // 4 % 4
    base = x
    for kk in range(1, 4):
        base = jnp.where(row == kk, pltpu.roll(x, PAD - kk, 1), base)
    rows_ref[...] = base.astype(BF).reshape(GROUPS, 16, PAD)

    @pl.loop(0, GROUPS)
    def _(g):
        some = rows_ref[g]
        for q in range(16):
            moved = some if q == 0 else pltpu.roll(some, PAD - 4 * q, 1)
            out_ref[g, q * 16 : (q + 1) * 16, :] = moved[:, :HALF]

    hot = one_hot(pick_ref[...], jnp.where((lane_ref[0] & 1) == 0, own_ref[0], own_ref[3]))
    for n in range(0, HALF, 256):
        base_ref[:, n : n + 256] = dot(hot, load_ref[:, n : n + 256])


def middle(lane_ref, pick_ref, own_ref, far_ref, base_ref, out_ref):
    hot = one_hot(pick_ref[...], jnp.where((lane_ref[0] & 1) == 0, own_ref[2], far_ref[:, HALF + BLOCK :]))
    for n in range(0, HALF, 256):
        out_ref[:, n : n + 256] = base_ref[:, n : n + 256] + dot(hot, far_ref[:, n : n + 256])


def correlate(lane_ref, pick_ref, own_ref, near_ref, base_ref, shift_ref, out_ref, sums_ref, flat_ref):
    hot = one_hot(pick_ref[...], jnp.where((lane_ref[0] & 1) == 0, own_ref[1], near_ref[:, HALF : HALF + BLOCK]))
    for n in range(0, HALF, 256):
        v = base_ref[:, n : n + 256] + dot(hot, near_ref[:, n : n + 256])
        top = v.astype(BF)
        rest = (v - top.astype(F32)).astype(BF)
        sums_ref[:, 0:64, n : n + 256] = top.reshape(GROUPS, 64, 256)
        sums_ref[:, 64:128, n : n + 256] = rest.reshape(GROUPS, 64, 256)
    r = lax.broadcasted_iota(jnp.int32, (64, 256), 0) // NBIN
    k = lax.broadcasted_iota(jnp.int32, (64, 256), 1) % 4
    for g in range(GROUPS):
        c = lax.dot_general(
            sums_ref[g], shift_ref[g], (((1,), (1,)), ((), ())), preferred_element_type=F32
        )
        c = jnp.where(r == k, (c[0:64] + c[64:128]) * (1.0 / S), 0.0).astype(BF)
        flat_ref[0, g * 32 : (g + 1) * 32, :] = c[0:32]
        flat_ref[1, g * 32 : (g + 1) * 32, :] = c[32:64]
    lag = lax.broadcasted_iota(jnp.int32, (256, 128), 0) // 4
    col = lax.broadcasted_iota(jnp.int32, (256, 128), 1)
    out = dot(flat_ref[0], (lag == col).astype(BF)) + dot(flat_ref[1], (lag + LAGS == col).astype(BF))
    out_ref[...] = out.astype(BF).reshape(2 * GROUPS, NBIN, 128)


def assemble(y_ref, out_ref):
    i = lax.broadcasted_iota(jnp.int32, (128, 256), 0)
    o = lax.broadcasted_iota(jnp.int32, (128, 256), 1)
    same = (i // LAGS) == (o // 128)
    early = jnp.logical_and(same, o % 128 == LAGS - 1 - i % LAGS).astype(BF)
    late = jnp.logical_and(same, o % 128 == LAGS + i % LAGS).astype(BF)
    out = dot(y_ref[0:8].reshape(128, 128), early) + dot(y_ref[8:16].reshape(128, 128), late)
    for q in range(2):
        out_ref[:, q] = out[:, q * 128 : (q + 1) * 128].reshape(8, NBIN, 128)


SCALAR = pl.BlockSpec(memory_space=pltpu.SMEM)
VMEM = pl.BlockSpec(memory_space=pltpu.VMEM)


def call(kernel, out, specs, scratch=(), flops=0):
    return pl.pallas_call(
        kernel,
        out_shape=[jax.ShapeDtypeStruct(shape, kind) for shape, kind in out],
        in_specs=specs,
        out_specs=[VMEM] * len(out),
        scratch_shapes=scratch,
        compiler_params=pltpu.CompilerParams(vmem_limit_bytes=20 << 20),
        cost_estimate=pl.CostEstimate(flops=flops, bytes_accessed=flops // 400, transcendentals=0),
        name=kernel.__name__,
    )


def on_device(waves, pair_bins, tile_perm):
    blk, lane = lax.axis_index("blk"), lax.axis_index("lane")
    core, y = blk % 2, lane % 2
    here = lane.reshape(1)

    load, full, own = call(
        prepare,
        [((BLOCK, WIDE), BF), ((BLOCK, S), BF), ((4, BLOCK, BLOCK), BF)],
        [SCALAR, VMEM, VMEM],
    )(here, waves, jnp.transpose(pair_bins, (1, 0, 2)))

    far = lax.ppermute(load, AXES, ACROSS)
    shifts, pick, base = call(
        early,
        [((GROUPS, 256, HALF), BF), ((ROWS, BLOCK), BF), ((ROWS, HALF), F32)],
        [SCALAR] * 3 + [VMEM] * 3,
        [pltpu.VMEM((GROUPS, 16, PAD), BF)],
        flops=1 << 32,
    )(here, blk.reshape(1), tile_perm, full, load, own)
    far, shifts, pick, base = lax.optimization_barrier((far, shifts, pick, base))

    near = lax.ppermute(jnp.where(core == y, load, far), AXES, PARTNER)
    (base,) = call(middle, [((ROWS, HALF), F32)], [SCALAR] + [VMEM] * 4, flops=1 << 29)(
        here, pick, own, far, base
    )
    near, base = lax.optimization_barrier((near, base))
    (mine,) = call(
        correlate,
        [((2 * GROUPS, NBIN, 128), BF)],
        [SCALAR] + [VMEM] * 5,
        [pltpu.VMEM((GROUPS, 128, HALF), BF), pltpu.VMEM((2, ROWS // 2, 256), BF)],
        flops=1 << 31,
    )(here, pick, own, near, base, shifts)

    mine = lax.all_to_all(mine, AXES, 0, 0, axis_index_groups=ROUND, tiled=True).astype(F32)
    mine = (mine[:16] + mine[16:]).astype(BF)
    mine = lax.ppermute(mine, AXES, TURN)
    (out,) = call(assemble, [((8, 2, NBIN, 128), F32)], [VMEM])(mine)
    return out.reshape(1, 16, NBIN, 128)


def solution(mesh):
    placed = (P("blk", None), P("blk", None, None), P("blk", None))
    return jax.shard_map(
        on_device,
        mesh=mesh,
        in_specs=placed,
        out_specs=P("blk", "lane", None, None),
        check_vma=False,
    )
```

```python
import jax
import jax.numpy as jnp
from jax import lax
from jax.experimental import pallas as pl
from jax.experimental.pallas import tpu as pltpu
from jax.sharding import PartitionSpec as P

S = 2048
LAGS = 64
NBIN = 16
STEPS = 3
BLOCK = 128
GROUPS = 16
ROWS = GROUPS * 64
HALF = S // 2
PAD = HALF + 128
WIDE = HALF + 2 * BLOCK
BF = jnp.bfloat16
F32 = jnp.float32
AXES = ("blk", "lane")


def device(z, h, core, x, y):
    return ((z % 8) * 8 + h * 2 + core) * 8 + x * 2 + y


PLACES = [
    (z, h, c, x, y)
    for z in range(8)
    for h in range(4)
    for c in range(2)
    for x in range(4)
    for y in range(2)
]


def beside(z, h, step):
    chip = (z * 4 + h + step) % 32
    return chip // 4, chip % 4


ACROSS = [
    (device(*pos), device(*beside(pos[0], pos[1], 1 if pos[4] else -1), pos[2], pos[3], 1 - pos[4]))
    for pos in PLACES
]
PARTNER = [(device(*pos), device(pos[0], pos[1], 1 - pos[2], pos[3], pos[4])) for pos in PLACES]


def ring(a, b, n):
    return min((a - b) % n, (b - a) % n)


OFFSETS = 0x72016534


def owner_z(z, x, y):
    near = ((x + 4 - (z >> 1)) & 3) * 2 + ((y + z) & 1)
    return (z + ((OFFSETS >> (4 * near)) & 7)) & 7


TURN = [
    (device(z, h, c, x, y), device(owner_z(z, x, y), h, c, z // 2, z % 2))
    for z, h, c, x, y in PLACES
]
ROUND = [
    [
        device(z, h, c, 2 * pair + x, y)
        for x in range(2)
        for y in range(2)
        for h in range(4)
        for c in range(2)
    ]
    for z in range(8)
    for pair in range(2)
]


def dot(a, b):
    return lax.dot_general(a, b, (((1,), (0,)), ((), ())), preferred_element_type=F32)


def prepare(lane_ref, waves_hbm, bins_hbm, load_ref, full_ref, own_ref, waves_ref, bins_ref, sems):
    parts = range(0, BLOCK, 32)
    copies = [
        pltpu.make_async_copy(waves_hbm.at[r : r + 32], waves_ref.at[r : r + 32], sems.at[i])
        for i, r in enumerate(parts)
    ]
    bins_copy = pltpu.make_async_copy(bins_hbm, bins_ref, sems.at[4])
    for copy in copies:
        copy.start()
    bins_copy.start()
    low = (lane_ref[0] & 2) == 0
    for i, r in enumerate(parts):
        copies[i].wait()
        w = waves_ref[r : r + 32, :]
        norm = jnp.sqrt(jnp.mean(w * w, axis=1, keepdims=True) + 1e-06)
        w = w / norm
        full_ref[r : r + 32, :] = w.astype(BF)
        load_ref[r : r + 32, :HALF] = jnp.where(low, w[:, :HALF], w[:, HALF:]).astype(BF)
    bins_copy.wait()
    for s in range(STEPS):
        b = bins_ref[s].astype(F32)
        turned = jnp.transpose(b).astype(BF)
        own_ref[s] = b.astype(BF)
        if s == 0:
            own_ref[STEPS] = turned
        else:
            load_ref[:, HALF + (s - 1) * BLOCK : HALF + s * BLOCK] = turned


def one_hot(pick, table):
    level = (lax.broadcasted_iota(jnp.int32, (ROWS, BLOCK), 0) % NBIN).astype(F32)
    return (dot(pick, table) == level).astype(BF)


def early(lane_ref, blk_ref, perm_ref, full_ref, load_ref, own_ref, out_ref, pick_ref, base_ref, rows_ref):
    def chosen(g, rows, which):
        at = which(lax.broadcasted_iota(jnp.int32, (rows, BLOCK), 0))
        first = 8 * owner_z(blk_ref[0] >> 3, ((lane_ref[0] >> 2) << 1) + g // 8, g // 4 % 2) + 2 * (g % 4)
        tiles = [perm_ref[0, first + own] * 2 for own in range(2)]
        node = [tiles[i % 2] + i // 2 for i in range(4)]
        want = jnp.where(at < 2, jnp.where(at == 0, node[0], node[1]), jnp.where(at == 2, node[2], node[3]))
        return (lax.broadcasted_iota(jnp.int32, (rows, BLOCK), 1) == want).astype(BF)

    for g in range(GROUPS):
        pick_ref[g * 64 : (g + 1) * 64, :] = chosen(g, 64, lambda r: r // NBIN)
    few = jnp.concatenate([chosen(g, 16, lambda r: r % 4) for g in range(GROUPS)], axis=0)
    x = dot(few, full_ref[...])
    x = jnp.concatenate([x, jnp.zeros((GROUPS * 16, 128), F32)], axis=1)
    x = jnp.where((lane_ref[0] & 1) == 0, pltpu.roll(x, LAGS - 1, 1), x)
    x = jnp.where((lane_ref[0] & 2) == 0, x[:, :PAD], x[:, HALF:])
    row = lax.broadcasted_iota(jnp.int32, (GROUPS * 16, PAD), 0) // 4 % 4
    base = x
    for kk in range(1, 4):
        base = jnp.where(row == kk, pltpu.roll(x, PAD - kk, 1), base)
    rows_ref[...] = base.astype(BF).reshape(GROUPS, 16, PAD)

    @pl.loop(0, GROUPS)
    def _(g):
        some = rows_ref[g]
        for q in range(16):
            moved = some if q == 0 else pltpu.roll(some, PAD - 4 * q, 1)
            out_ref[g, q * 16 : (q + 1) * 16, :] = moved[:, :HALF]

    hot = one_hot(pick_ref[...], jnp.where((lane_ref[0] & 1) == 0, own_ref[0], own_ref[3]))
    for n in range(0, HALF, 256):
        base_ref[:, n : n + 256] = dot(hot, load_ref[:, n : n + 256])


def middle(lane_ref, pick_ref, own_ref, far_ref, base_ref, out_ref):
    hot = one_hot(pick_ref[...], jnp.where((lane_ref[0] & 1) == 0, own_ref[2], far_ref[:, HALF + BLOCK :]))
    for n in range(0, HALF, 256):
        out_ref[:, n : n + 256] = base_ref[:, n : n + 256] + dot(hot, far_ref[:, n : n + 256])


def correlate(lane_ref, pick_ref, own_ref, near_ref, base_ref, shift_ref, out_ref, sums_ref, flat_ref):
    hot = one_hot(pick_ref[...], jnp.where((lane_ref[0] & 1) == 0, own_ref[1], near_ref[:, HALF : HALF + BLOCK]))
    for n in range(0, HALF, 256):
        v = base_ref[:, n : n + 256] + dot(hot, near_ref[:, n : n + 256])
        top = v.astype(BF)
        rest = (v - top.astype(F32)).astype(BF)
        sums_ref[:, 0:64, n : n + 256] = top.reshape(GROUPS, 64, 256)
        sums_ref[:, 64:128, n : n + 256] = rest.reshape(GROUPS, 64, 256)
    r = lax.broadcasted_iota(jnp.int32, (64, 256), 0) // NBIN
    k = lax.broadcasted_iota(jnp.int32, (64, 256), 1) % 4
    for g in range(GROUPS):
        c = lax.dot_general(
            sums_ref[g], shift_ref[g], (((1,), (1,)), ((), ())), preferred_element_type=F32
        )
        c = jnp.where(r == k, (c[0:64] + c[64:128]) * (1.0 / S), 0.0).astype(BF)
        flat_ref[0, g * 32 : (g + 1) * 32, :] = c[0:32]
        flat_ref[1, g * 32 : (g + 1) * 32, :] = c[32:64]
    lag = lax.broadcasted_iota(jnp.int32, (256, 128), 0) // 4
    col = lax.broadcasted_iota(jnp.int32, (256, 128), 1)
    out = dot(flat_ref[0], (lag == col).astype(BF)) + dot(flat_ref[1], (lag + LAGS == col).astype(BF))
    out_ref[...] = out.astype(BF).reshape(2 * GROUPS, NBIN, 128)


def assemble(y_ref, out_ref):
    i = lax.broadcasted_iota(jnp.int32, (128, 256), 0)
    o = lax.broadcasted_iota(jnp.int32, (128, 256), 1)
    same = (i // LAGS) == (o // 128)
    early = jnp.logical_and(same, o % 128 == LAGS - 1 - i % LAGS).astype(BF)
    late = jnp.logical_and(same, o % 128 == LAGS + i % LAGS).astype(BF)
    out = dot(y_ref[0:8].reshape(128, 128), early) + dot(y_ref[8:16].reshape(128, 128), late)
    for q in range(2):
        out_ref[:, q] = out[:, q * 128 : (q + 1) * 128].reshape(8, NBIN, 128)


SCALAR = pl.BlockSpec(memory_space=pltpu.SMEM)
HBM = pl.BlockSpec(memory_space=pltpu.HBM)
VMEM = pl.BlockSpec(memory_space=pltpu.VMEM)


def call(kernel, out, specs, scratch=(), flops=0, mib=20):
    return pl.pallas_call(
        kernel,
        out_shape=[jax.ShapeDtypeStruct(shape, kind) for shape, kind in out],
        in_specs=specs,
        out_specs=[VMEM] * len(out),
        scratch_shapes=scratch,
        compiler_params=pltpu.CompilerParams(vmem_limit_bytes=mib << 20),
        cost_estimate=pl.CostEstimate(flops=flops, bytes_accessed=flops // 400, transcendentals=0),
        name=kernel.__name__,
    )


def on_device(waves, pair_bins, tile_perm):
    blk, lane = lax.axis_index("blk"), lax.axis_index("lane")
    core, y = blk % 2, lane % 2
    here = lane.reshape(1)

    load, full, own = call(
        prepare,
        [((BLOCK, WIDE), BF), ((BLOCK, S), BF), ((4, BLOCK, BLOCK), BF)],
        [SCALAR, HBM, HBM],
        [pltpu.VMEM((BLOCK, S), F32), pltpu.VMEM((STEPS, BLOCK, BLOCK), jnp.int32), pltpu.SemaphoreType.DMA((5,))],
        mib=52,
    )(here, waves, jnp.transpose(pair_bins, (1, 0, 2)))

    far = lax.ppermute(load, AXES, ACROSS)
    shifts, pick, base = call(
        early,
        [((GROUPS, 256, HALF), BF), ((ROWS, BLOCK), BF), ((ROWS, HALF), F32)],
        [SCALAR] * 3 + [VMEM] * 3,
        [pltpu.VMEM((GROUPS, 16, PAD), BF)],
        flops=1 << 32,
    )(here, blk.reshape(1), tile_perm, full, load, own)
    far, shifts, pick, base = lax.optimization_barrier((far, shifts, pick, base))

    used = HALF + BLOCK
    near = lax.ppermute(jnp.where(core == y, load[:, :used], far[:, :used]), AXES, PARTNER)
    (base,) = call(middle, [((ROWS, HALF), F32)], [SCALAR] + [VMEM] * 4, flops=1 << 29)(
        here, pick, own, far, base
    )
    near, base = lax.optimization_barrier((near, base))
    (mine,) = call(
        correlate,
        [((2 * GROUPS, NBIN, 128), BF)],
        [SCALAR] + [VMEM] * 5,
        [pltpu.VMEM((GROUPS, 128, HALF), BF), pltpu.VMEM((2, ROWS // 2, 256), BF)],
        flops=1 << 31,
    )(here, pick, own, near, base, shifts)

    mine = lax.all_to_all(mine, AXES, 0, 0, axis_index_groups=ROUND, tiled=True).astype(F32)
    mine = (mine[:16] + mine[16:]).astype(BF)
    mine = lax.ppermute(mine, AXES, TURN)
    (out,) = call(assemble, [((8, 2, NBIN, 128), F32)], [VMEM])(mine)
    return out.reshape(1, 16, NBIN, 128)


def solution(mesh):
    placed = (P("blk", None), P("blk", None, None), P("blk", None))
    return jax.shard_map(
        on_device,
        mesh=mesh,
        in_specs=placed,
        out_specs=P("blk", "lane", None, None),
        check_vma=False,
    )
```
